256 devices in a mesh: depth: 8 (over z_hi, y), lat: 32 (over z_lo, x, core).
Axes of the slice: x: 4, y: 4, z: 8 (z_hi: 2, z_lo: 4; z = z_hi * 4 + z_lo), core: 2. Of those that a mesh axis runs over, the one named last changes fastest.
Arguments:
- down_state: bfloat16 [8, 192, 65536], P('depth', None, 'lat'), may hold values from -6 to 6
- up_state: bfloat16 [8, 192, 65536], P('depth', None, 'lat'), may hold values from -6 to 6
- reflectivity: float32 [8, 65536], P('depth', 'lat'), may hold values from -0.3 to 0.3
- w_down: bfloat16 [8, 32, 2048, 1024], P('depth', 'lat'), may hold values from -0.125 to 0.125
- w_up: bfloat16 [8, 32, 2048, 1024], P('depth', 'lat'), may hold values from -0.125 to 0.125
Outputs:
- down_final: bfloat16 [8, 192, 65536], P('depth', None, 'lat')
- up_final: bfloat16 [8, 192, 65536], P('depth', None, 'lat')
The draws below stay inside these ranges and needn't reach their ends.
All inputs are finite; a program needn't handle non-finite values.
Results may differ from the reference program's by a relative error of at most 0.0086.
Values may be sent and summed in bfloat16 or wider, within the bound.
No kernel may reach another device: no remote copies, remote signals or barrier semaphores. Data moves between devices by JAX's collectives and lax.ppermute only.
A program may use at most 64 MiB of HBM per device.

```python
import jax
import jax.numpy as jnp
from jax import lax

BLOCK = 1024
HALO = 512
COLS = 192
TICKS = 4
WINDOW = 2048
TILES = 32
LATERAL = 65536
DEPTHS = 8


def level_of(stream_key, dims, pieces, smallest, largest):
    def one(position, shards_of):
        draws = jax.random.uniform(jax.random.fold_in(jax.random.fold_in(stream_key, 6), position), (shards_of,), jnp.float32, smallest / len(pieces), largest / len(pieces))
        return jnp.repeat(jnp.exp(draws), dims[position] // shards_of).reshape((-1,) + (1,) * (len(dims) - position - 1))

    factor_of = one(*pieces[0])
    for cut in pieces[1:]:
        factor_of = factor_of * one(*cut)
    return factor_of


def normal_values(own_key, shape, scale, limit, pieces=(), kind=jnp.bfloat16):
    entries = jax.random.normal(own_key, shape, jnp.float32) * scale
    if len(pieces) > 0:
        entries = level_of(own_key, shape, pieces, -0.22, 0.18) * entries
    return jnp.clip(entries, min=-limit, max=limit).astype(kind)


def setup_inputs(seed: int = 0) -> dict:
    keys = jax.random.split(jax.random.key(seed), 6)
    down_state = normal_values(keys[0], (DEPTHS, COLS, LATERAL), 1.0, 6.0, ((0, 8), (2, 32)))
    up_state = normal_values(keys[1], (DEPTHS, COLS, LATERAL), 1.0, 6.0, ((0, 8), (2, 32)))
    reflectivity = jnp.clip(jax.random.uniform(keys[2], (DEPTHS, LATERAL), jnp.float32, -0.3, 0.3) * level_of(keys[2], (DEPTHS, LATERAL), ((0, 8), (1, 32)), -0.4, 0.0), -0.3, 0.3)
    w_down = normal_values(keys[3], (DEPTHS, TILES, WINDOW, BLOCK), WINDOW ** -0.5, 0.125, ((0, 8), (1, 32)))
    w_up = normal_values(keys[4], (DEPTHS, TILES, WINDOW, BLOCK), WINDOW ** -0.5, 0.125, ((0, 8), (1, 32)))
    return dict(down_state=down_state, up_state=up_state, reflectivity=reflectivity, w_down=w_down, w_up=w_up)


def extrapolate(mixed, weight):
    levels, columns, points = mixed.shape
    block_count = points // BLOCK
    tile_count = weight.shape[1]
    centre_part = mixed.reshape(levels, columns, block_count, BLOCK)
    zero_rim = jnp.zeros((levels, columns, 1, HALO), mixed.dtype)
    left_rim = jnp.concatenate([zero_rim, centre_part[:, :, :-1, BLOCK - HALO:]], axis=2)
    right_rim = jnp.concatenate([centre_part[:, :, 1:, :HALO], zero_rim], axis=2)
    windows = jnp.concatenate([left_rim, centre_part, right_rim], axis=3)
    windows = windows.reshape(levels, columns, tile_count, block_count // tile_count, WINDOW)

    def per_level(operands):
        window_rows, level_weight = operands
        return jnp.einsum("ctbw,two->ctbo", window_rows.astype(jnp.float32), level_weight.astype(jnp.float32), precision=lax.Precision.HIGHEST)

    product = lax.map(per_level, (windows, weight))
    return product.reshape(levels, columns, points)


def reference(down_state, up_state, reflectivity, w_down, w_up):
    reflect_col = reflectivity[:, None, :]
    going_down, going_up = down_state, up_state
    for tick_index in range(TICKS):
        down_wide = going_down.astype(jnp.float32)
        up_wide = going_up.astype(jnp.float32)
        mixed_down = ((1.0 + reflect_col) * down_wide - reflect_col * up_wide).astype(jnp.bfloat16)
        mixed_up = ((1.0 - reflect_col) * up_wide + reflect_col * down_wide).astype(jnp.bfloat16)
        out_down = extrapolate(mixed_down, w_down).astype(jnp.bfloat16)
        out_up = extrapolate(mixed_up, w_up).astype(jnp.bfloat16)
        going_down = jnp.concatenate([-out_up[:1], out_down[:-1]], axis=0)
        going_up = jnp.concatenate([out_up[1:], jnp.zeros_like(out_up[:1])], axis=0)
    return going_down, going_up
```

```python
import functools

import jax
import jax.numpy as jnp
from jax import lax
from jax.experimental import pallas as pl
from jax.experimental.pallas import tpu as pltpu
from jax.sharding import PartitionSpec as P

BLOCK = 1024
HALO = 512
TICKS = 4
CHUNKS = ((192, 80),)

SPLIT_EDGE = True
VMEM = pl.BlockSpec(memory_space=pltpu.VMEM)
SMEM = pl.BlockSpec(memory_space=pltpu.SMEM)


def swap(*pairs):
    return [q for a, b in pairs for q in ((a, b), (b, a))]


INNER = swap((1, 2), (5, 6))
FIRST_DIRECT = INNER + swap((3, 4))
FIRST_STEP = INNER + [(3, 0), (4, 7)]
FIRST_FORWARD = [(0, 4), (7, 3)]
SECOND = swap((0, 1), (2, 3), (4, 5), (6, 7))


def call(body, outs, ins, name):
    many = isinstance(outs, (tuple, list))
    return pl.pallas_call(
        body,
        out_shape=outs,
        in_specs=[SMEM] + [VMEM] * (len(ins) - 1),
        out_specs=tuple(VMEM for _ in outs) if many else VMEM,
        compiler_params=pltpu.CompilerParams(vmem_limit_bytes=20 * 1024 * 1024),
        cost_estimate=pl.CostEstimate(flops=1, transcendentals=0, bytes_accessed=1),
        name=name,
    )(*ins)


def store_mixed(scal, sign, first, second, reflect, m_ref, e1_ref, e2_ref, rows):
    rho = reflect * jnp.where(scal[0] == 1, 1.0, -1.0)
    first = first.astype(jnp.float32)
    second = second.astype(jnp.float32)
    mixed = (
        (1.0 + rho) * first - (rho * sign) * second,
        ((1.0 - rho) * sign) * second + rho * first,
    )
    size = mixed[0].shape[1]
    for f in range(2):
        value = mixed[f].astype(jnp.bfloat16)
        m_ref[f, rows, :] = value
        head = value[:, :HALO]
        tail = value[:, size - HALO :]
        even = scal[2] == 0
        e1_ref[f, rows, :] = jnp.where(even, tail, head)
        e2_ref[f, rows, :] = jnp.where(even, head, tail)


def mix_start(scal, down, up, reflect, m_ref, e1_ref, e2_ref):
    odd = scal[0] == 1
    first = jnp.where(odd, down[...], up[...])
    second = jnp.where(odd, up[...], down[...])
    store_mixed(scal, 1.0, first, second, reflect[...], m_ref, e1_ref, e2_ref, slice(None))


def second_parts(scal, own_direct, own_step, got_direct, got_step, got_forward):
    level = scal[1]
    direct = jnp.where(level == 0, own_direct[...], got_direct[...])
    step = jnp.where(
        level == 0,
        own_step[...],
        jnp.where(
            (level == 3) | (level == 4),
            got_forward[...],
            jnp.where(level == 7, jnp.zeros_like(got_step[...]), got_step[...]),
        ),
    )
    return direct, step


def mix_next(scal, first, own_direct, own_step, got_direct, got_step, got_forward, reflect, m_ref, e1_ref, e2_ref):
    sign = jnp.where(scal[1] == 0, -1.0, 1.0)
    direct, step = second_parts(scal, own_direct, own_step, got_direct, got_step, got_forward)
    cut = direct.shape[0]
    rows = first.shape[0]
    value = first[...]
    store_mixed(scal, sign, value[:cut], direct, reflect[...], m_ref, e1_ref, e2_ref, pl.ds(0, cut))
    store_mixed(scal, sign, value[cut:], step, reflect[...], m_ref, e1_ref, e2_ref, pl.ds(cut, rows - cut))


def load_weights(scal, order, w_down, w_up, out, sems):
    del order

    def both(*sources):
        copies = [pltpu.make_async_copy(w.at[0, 0], out.at[f], sems.at[f]) for f, w in enumerate(sources)]
        for copy in copies:
            copy.start()
        for copy in copies:
            copy.wait()

    @pl.when(scal[0] == 1)
    def _():
        both(w_down, w_up)

    @pl.when(scal[0] == 0)
    def _():
        both(w_up, w_down)


def weights_by_role(scal, order, w_down, w_up):
    return pl.pallas_call(
        load_weights,
        out_shape=jax.ShapeDtypeStruct((2, 2 * BLOCK, BLOCK), jnp.bfloat16),
        in_specs=[SMEM] + [pl.BlockSpec(memory_space=pl.ANY)] * 3,
        out_specs=VMEM,
        scratch_shapes=[pltpu.SemaphoreType.DMA((2,))],
        compiler_params=pltpu.CompilerParams(vmem_limit_bytes=20 * 1024 * 1024),
        cost_estimate=pl.CostEstimate(flops=1, transcendentals=0, bytes_accessed=1),
        name="weights",
    )(scal, order, w_down, w_up)


def body_dots(scal, m_ref, w_ref, acc_ref):
    for f in range(2):
        left = jnp.concatenate([m_ref[f, :, :BLOCK], m_ref[f, :, BLOCK:]], axis=0)
        acc_ref[f] = jnp.dot(
            left, w_ref[f, HALO : HALO + BLOCK, :], preferred_element_type=jnp.float32
        )


def edge_dots(scal, m_ref, h1_ref, h2_ref, acc_ref, w_ref, *outs, fields):
    even = scal[2] == 0
    for field, parts in zip(fields, outs if len(fields) == 1 else (outs[:2], outs[2:])):
        parts = outs if len(fields) == 1 else parts
        h1 = h1_ref[field]
        h2 = h2_ref[field]
        from_left = jnp.where(even, h2, h1)
        from_right = jnp.where(even, h1, h2)
        columns = h1.shape[0]
        low = jnp.concatenate([from_left, m_ref[field, :, HALO:BLOCK]], axis=0)
        high = jnp.concatenate([m_ref[field, :, BLOCK : BLOCK + HALO], from_right], axis=0)
        summed = (
            acc_ref[field]
            + jnp.dot(low, w_ref[field, :HALO, :], preferred_element_type=jnp.float32)
            + jnp.dot(high, w_ref[field, HALO + BLOCK :, :], preferred_element_type=jnp.float32)
        ).astype(jnp.bfloat16)
        start = 0
        for out in parts:
            rows = out.shape[0]
            out[:, :BLOCK] = summed[start : start + rows]
            out[:, BLOCK:] = summed[columns + start : columns + start + rows]
            start += rows


def finish(scal, *refs):
    down_ref, up_ref = refs[-2:]
    sign = jnp.where(scal[1] == 0, -1.0, 1.0).astype(jnp.bfloat16)
    odd = scal[0] == 1
    start = 0
    for c in range(len(CHUNKS)):
        first, *rest = refs[6 * c : 6 * c + 6]
        for part in second_parts(scal, *rest):
            rows = part.shape[0]
            one = first[pl.ds(start - sum(n for n, _ in CHUNKS[:c]), rows), :]
            two = part * sign
            down_ref[0, pl.ds(start, rows), :] = jnp.where(odd, one, two)
            up_ref[0, pl.ds(start, rows), :] = jnp.where(odd, two, one)
            start += rows


def on_device(down_state, up_state, reflectivity, w_down, w_up):
    level = lax.axis_index("depth")
    tile = lax.axis_index("lat")
    tiles = lax.axis_size("lat")
    scal = jnp.stack([level % 2, level, tile % 2]).astype(jnp.int32)
    inside = swap(*[(i, i + 1) for i in range(0, tiles, 2)])
    outside = swap(*[(i, i + 1) for i in range(1, tiles - 1, 2)])
    wide = down_state.shape[2]
    bf = lambda *s: jax.ShapeDtypeStruct(s, jnp.bfloat16)
    state = []
    start = 0
    for n, _ in CHUNKS:
        state.append((down_state[0, start : start + n], up_state[0, start : start + n]))
        start += n
    weights = None
    for tick in range(TICKS):
        for c, (n, k) in enumerate(CHUNKS):
            m, e1, e2 = call(
                mix_start if tick == 0 else mix_next,
                (bf(2, n, wide), bf(2, n, HALO), bf(2, n, HALO)),
                (scal, *state[c], reflectivity),
                "mix",
            )
            h2 = lax.ppermute(e2, "lat", outside)
            h1 = lax.ppermute(e1, "lat", inside)
            if weights is None:
                weights = weights_by_role(scal, m, w_down, w_up)
            acc = call(
                body_dots,
                jax.ShapeDtypeStruct((2, 2 * n, BLOCK), jnp.float32),
                (scal, m, weights),
                "body",
            )
            if SPLIT_EDGE:
                own = call(
                    functools.partial(edge_dots, fields=(0,)),
                    (bf(n - k, wide), bf(k, wide)),
                    (scal, m, h1, h2, acc, weights),
                    "edge0",
                )
                (other,) = call(
                    functools.partial(edge_dots, fields=(1,)),
                    (bf(n, wide),),
                    (scal, m, h1, h2, acc, weights),
                    "edge1",
                )
            else:
                *own, other = call(
                    functools.partial(edge_dots, fields=(0, 1)),
                    (bf(n - k, wide), bf(k, wide), bf(n, wide)),
                    (scal, m, h1, h2, acc, weights),
                    "edges",
                )
            got_direct = lax.ppermute(own[0], "depth", FIRST_DIRECT)
            got_step = lax.ppermute(own[1], "depth", FIRST_STEP)
            first = lax.ppermute(other, "depth", SECOND)
            got_forward = lax.ppermute(got_step, "depth", FIRST_FORWARD)
            state[c] = (first, *own, got_direct, got_step, got_forward)
    total = sum(n for n, _ in CHUNKS)
    return call(
        finish,
        (bf(1, total, wide), bf(1, total, wide)),
        (scal, *[x for s in state for x in s]),
        "finish",
    )


def solution(mesh):
    in_specs = (
        P("depth", None, "lat"),
        P("depth", None, "lat"),
        P("depth", "lat"),
        P("depth", "lat", None, None),
        P("depth", "lat", None, None),
    )
    out_specs = (P("depth", None, "lat"), P("depth", None, "lat"))
    return jax.shard_map(
        on_device, mesh=mesh, in_specs=in_specs, out_specs=out_specs, check_vma=False
    )
```

```python
import functools

import jax
import jax.numpy as jnp
from jax import lax
from jax.experimental import pallas as pl
from jax.experimental.pallas import tpu as pltpu
from jax.sharding import PartitionSpec as P

BLOCK = 1024
HALO = 512
TICKS = 4
STEP_ROWS = 64
HFLIP = False
GRANT = 20 * 1024 * 1024
HINT = 10_000_000_000

VMEM = pl.BlockSpec(memory_space=pltpu.VMEM)
SMEM = pl.BlockSpec(memory_space=pltpu.SMEM)
HBM = pl.BlockSpec(memory_space=pltpu.HBM)


def swap(*pairs):
    return [q for a, b in pairs for q in ((a, b), (b, a))]


INNER = swap((1, 2), (5, 6))
FIRST_DIRECT = INNER + swap((3, 4))
FIRST_STEP = INNER + [(3, 0), (4, 7)]
FIRST_FORWARD = [(0, 4), (7, 3)]
SECOND = swap((0, 1), (2, 3), (4, 5), (6, 7))


def bf(*shape):
    return jax.ShapeDtypeStruct(shape, jnp.bfloat16)


def f32(*shape):
    return jax.ShapeDtypeStruct(shape, jnp.float32)


def call(body, outs, ins, name, specs=None, scratch=(), out_specs=None, aliases=None):
    return pl.pallas_call(
        body,
        out_shape=tuple(outs),
        in_specs=[SMEM] + (specs or [VMEM] * (len(ins) - 1)),
        out_specs=out_specs or tuple(VMEM for _ in outs),
        scratch_shapes=scratch,
        input_output_aliases=aliases or {},
        compiler_params=pltpu.CompilerParams(vmem_limit_bytes=GRANT),
        cost_estimate=pl.CostEstimate(flops=HINT, transcendentals=0, bytes_accessed=1),
        name=name,
    )(*ins)


def mixed(rho, sign, first, second):
    first = first.astype(jnp.float32)
    second = second.astype(jnp.float32)
    return (
        ((1.0 + rho) * first - (rho * sign) * second).astype(jnp.bfloat16),
        (((1.0 - rho) * sign) * second + rho * first).astype(jnp.bfloat16),
    )


def rho_of(scal, reflect):
    return reflect * jnp.where(scal[0] == 1, 1.0, -1.0)


def sign_of(scal):
    return jnp.where(scal[1] == 0, -1.0, 1.0)


def second_parts(scal, own_direct, own_step, got_direct, got_step, got_forward, cut=slice(None)):
    level = scal[1]
    direct = jnp.where(level == 0, own_direct[:, cut], got_direct[:, cut])
    step = jnp.where((level == 3) | (level == 4), got_forward[:, cut], got_step[:, cut])
    step = jnp.where(level == 7, jnp.zeros_like(step), step)
    return direct, jnp.where(level == 0, own_step[:, cut], step)


def ends_next(scal, first, *refs):
    second = refs[:5]
    reflect, e1_ref, e2_ref = refs[5:]
    size = first.shape[1]
    rho = rho_of(scal, reflect[...])
    sign = sign_of(scal)
    for cut in (slice(0, HALO), slice(size - HALO, size)):
        goes_first = (scal[2] == 0) == (cut.start > 0)
        start = 0
        for part in second_parts(scal, *second, cut=cut):
            rows = pl.ds(start, part.shape[0])
            pair = mixed(rho[:, cut], sign, first[rows, cut], part)

            @pl.when(goes_first)
            def _():
                for f in range(2):
                    e1_ref[f, rows, :] = pair[f]

            @pl.when(jnp.logical_not(goes_first))
            def _():
                for f in range(2):
                    e2_ref[f, rows, :] = pair[f]

            start += part.shape[0]


def ends_start(scal, down, up, reflect, e1_ref, e2_ref, ends_ref, r_ref, sems):
    odd = scal[0] == 1
    even_tile = scal[2] == 0
    size = down.shape[2]
    cuts = (slice(0, HALO), slice(size - HALO, size))
    copies = [pltpu.make_async_copy(reflect, r_ref, sems.at[4])]
    for i, state in enumerate((down, up)):
        for j, cut in enumerate(cuts):
            source = state.at[0, :, pl.ds(cut.start, HALO)]
            copies.append(pltpu.make_async_copy(source, ends_ref.at[i, j], sems.at[2 * i + j]))
    for copy in copies:
        copy.start()
    for copy in copies:
        copy.wait()
    rho = rho_of(scal, r_ref[...])
    for j, cut in enumerate(cuts):
        one, two = ends_ref[0, j], ends_ref[1, j]
        pair = mixed(rho[:, cut], 1.0, jnp.where(odd, one, two), jnp.where(odd, two, one))
        goes_first = even_tile == (j == 1)

        @pl.when(goes_first)
        def _():
            for f in range(2):
                e1_ref[f] = pair[f]

        @pl.when(jnp.logical_not(goes_first))
        def _():
            for f in range(2):
                e2_ref[f] = pair[f]


def dot(left, right):
    return jnp.dot(left, right, preferred_element_type=jnp.float32)


def inner_dots(m_ref, w_ref, acc_ref, f):
    columns = m_ref.shape[1]
    left = jnp.concatenate([m_ref[f, :, :BLOCK], m_ref[f, :, BLOCK:]], axis=0)
    both = dot(left, w_ref[f, HALO : HALO + BLOCK, :])
    acc_ref[f, :columns] = both[:columns] + dot(m_ref[f, :, BLOCK : BLOCK + HALO], w_ref[f, HALO + BLOCK :, :])
    acc_ref[f, columns:] = both[columns:] + dot(m_ref[f, :, HALO:BLOCK], w_ref[f, :HALO, :])


def body_start(scal, down, up, reflect, w_down, w_up, acc_ref, w_ref, m_ref, sems):
    odd = scal[0] == 1

    def copies(*sources):
        return [pltpu.make_async_copy(w.at[0, 0], w_ref.at[f], sems.at[f]) for f, w in enumerate(sources)]

    @pl.when(odd)
    def _():
        for copy in copies(w_down, w_up):
            copy.start()

    @pl.when(jnp.logical_not(odd))
    def _():
        for copy in copies(w_up, w_down):
            copy.start()

    one, two = down[0], up[0]
    pair = mixed(rho_of(scal, reflect[...]), 1.0, jnp.where(odd, one, two), jnp.where(odd, two, one))
    for f in range(2):
        m_ref[f] = pair[f]
    for f, copy in enumerate(copies(w_down, w_up)):
        copy.wait()
        inner_dots(m_ref, w_ref, acc_ref, f)


def body_next(scal, first, *refs):
    reflect, w_ref, acc_ref, m_ref = refs[5:]
    rho = rho_of(scal, reflect[...])
    start = 0
    for part in second_parts(scal, *refs[:5]):
        rows = pl.ds(start, part.shape[0])
        pair = mixed(rho, sign_of(scal), first[rows, :], part)
        for f in range(2):
            m_ref[f, rows, :] = pair[f]
        start += part.shape[0]
    for f in range(2):
        inner_dots(m_ref, w_ref, acc_ref, f)


def halo_dots(scal, h1_ref, h2_ref, acc_ref, w_ref, *outs):
    even = scal[2] == 0
    for f, parts in ((0, outs[:2]), (1, outs[2:])):
        h1 = h1_ref[f]
        h2 = h2_ref[f]
        columns = h1.shape[0]
        left = acc_ref[f, :columns] + dot(jnp.where(even, h2, h1), w_ref[f, :HALO, :])
        right = acc_ref[f, columns:] + dot(jnp.where(even, h1, h2), w_ref[f, HALO + BLOCK :, :])
        start = 0
        for out in parts:
            rows = out.shape[0]
            out[:, :BLOCK] = left[start : start + rows].astype(jnp.bfloat16)
            out[:, BLOCK:] = right[start : start + rows].astype(jnp.bfloat16)
            start += rows


def finish(scal, first, *refs):
    down_ref, up_ref = refs[-2:]
    sign = sign_of(scal).astype(jnp.bfloat16)
    odd = scal[0] == 1
    start = 0
    for part in second_parts(scal, *refs[:-2]):
        rows = pl.ds(start, part.shape[0])
        one = first[rows, :]
        two = part * sign
        down_ref[0, rows, :] = jnp.where(odd, one, two)
        up_ref[0, rows, :] = jnp.where(odd, two, one)
        start += part.shape[0]


def on_device(down_state, up_state, reflectivity, w_down, w_up):
    level = lax.axis_index("depth")
    tile = lax.axis_index("lat")
    tiles = lax.axis_size("lat")
    columns, wide = down_state.shape[1:]
    scal = jnp.stack([level % 2, level, tile % 2]).astype(jnp.int32)
    inside = swap(*[(i, i + 1) for i in range(0, tiles, 2)])
    outside = swap(*[(i, i + 1) for i in range(1, tiles - 1, 2)])
    far = [pltpu.with_memory_space_constraint(x, pltpu.HBM) for x in (down_state, up_state, reflectivity, w_down, w_up)]
    sums = f32(2, 2 * columns, BLOCK)
    fields = pltpu.VMEM((2, columns, wide), jnp.bfloat16)
    for tick in range(TICKS):
        if tick == 0:
            e1, e2 = call(
                ends_start,
                (bf(2, columns, HALO),) * 2,
                (scal, *far[:3]),
                "ends",
                specs=[HBM] * 3,
                scratch=[
                    pltpu.VMEM((2, 2, columns, HALO), jnp.bfloat16),
                    pltpu.VMEM((1, wide), jnp.float32),
                    pltpu.SemaphoreType.DMA((5,)),
                ],
            )
        else:
            e1, e2 = call(ends_next, (bf(2, columns, HALO),) * 2, (scal, first, *second, reflectivity), "ends")
        if HFLIP and tick:
            h1 = lax.ppermute(e1, "lat", inside)
            h2 = lax.ppermute(e2, "lat", outside)
        else:
            h2 = lax.ppermute(e2, "lat", outside)
            h1 = lax.ppermute(e1, "lat", inside)
        if tick == 0:
            acc, weights = call(
                body_start,
                (sums, bf(2, 2 * BLOCK, BLOCK)),
                (scal, down_state, up_state, reflectivity, *far[3:]),
                "body",
                specs=[VMEM] * 3 + [HBM] * 2,
                scratch=[fields, pltpu.SemaphoreType.DMA((2,))],
            )
        else:
            (acc,) = call(body_next, (sums,), (scal, first, *second, reflectivity, weights), "body", scratch=[fields])
        *own, other = call(
            halo_dots,
            (bf(columns - STEP_ROWS, wide), bf(STEP_ROWS, wide), bf(columns, wide)),
            (scal, h1, h2, acc, weights),
            "edges",
        )
        first = lax.ppermute(other, "depth", SECOND)
        got_step = lax.ppermute(own[1], "depth", FIRST_STEP)
        got_direct = lax.ppermute(own[0], "depth", FIRST_DIRECT)
        got_forward = lax.ppermute(got_step, "depth", FIRST_FORWARD)
        second = (*own, got_direct, got_step, got_forward)
    return call(finish, (bf(1, columns, wide),) * 2, (scal, first, *second), "finish")


def solution(mesh):
    in_specs = (
        P("depth", None, "lat"),
        P("depth", None, "lat"),
        P("depth", "lat"),
        P("depth", "lat", None, None),
        P("depth", "lat", None, None),
    )
    out_specs = (P("depth", None, "lat"), P("depth", None, "lat"))
    return jax.shard_map(
        on_device, mesh=mesh, in_specs=in_specs, out_specs=out_specs, check_vma=False
    )
```

```python
import functools

import jax
import jax.numpy as jnp
from jax import lax
from jax.experimental import pallas as pl
from jax.experimental.pallas import tpu as pltpu
from jax.sharding import PartitionSpec as P

BLOCK = 1024
HALO = 512
STEP_ROWS = (80, 64, 64, 80)
GRANT = 20 * 1024 * 1024
HINT = 10_000_000_000

VMEM = pl.BlockSpec(memory_space=pltpu.VMEM)
HBM = pl.BlockSpec(memory_space=pltpu.HBM)


def swap(*pairs):
    return [q for a, b in pairs for q in ((a, b), (b, a))]


INNER = swap((1, 2), (5, 6))
FIRST_DIRECT = INNER + swap((3, 4))
FIRST_STEP = INNER + [(3, 0), (4, 7)]
FIRST_FORWARD = [(0, 4), (7, 3)]
SECOND = swap((0, 1), (2, 3), (4, 5), (6, 7))


def bf(*shape):
    return jax.ShapeDtypeStruct(shape, jnp.bfloat16)


def f32(*shape):
    return jax.ShapeDtypeStruct(shape, jnp.float32)


def call(body, outs, ins, name, specs=None, scratch=(), out_specs=None, aliases=None):
    def kernel(*refs):
        level = lax.axis_index("depth")
        body((level % 2, level, lax.axis_index("lat") % 2), *refs)

    return pl.pallas_call(
        kernel,
        out_shape=tuple(outs),
        in_specs=specs or [VMEM] * len(ins),
        out_specs=out_specs or tuple(VMEM for _ in outs),
        scratch_shapes=scratch,
        input_output_aliases=aliases or {},
        compiler_params=pltpu.CompilerParams(vmem_limit_bytes=GRANT),
        cost_estimate=pl.CostEstimate(flops=HINT, transcendentals=0, bytes_accessed=1),
        name=name,
    )(*ins)


def mixed(rho, sign, first, second):
    first = first.astype(jnp.float32)
    second = second.astype(jnp.float32)
    return (
        ((1.0 + rho) * first - (rho * sign) * second).astype(jnp.bfloat16),
        (((1.0 - rho) * sign) * second + rho * first).astype(jnp.bfloat16),
    )


def rho_of(scal, reflect):
    return reflect * jnp.where(scal[0] == 1, 1.0, -1.0)


def sign_of(scal):
    return jnp.where(scal[1] == 0, -1.0, 1.0)


def second_parts(scal, own_direct, own_step, got_direct, got_step, got_forward, cut=slice(None)):
    level = scal[1]
    direct = jnp.where(level == 0, own_direct[:, cut], got_direct[:, cut])
    step = jnp.where((level == 3) | (level == 4), got_forward[:, cut], got_step[:, cut])
    step = jnp.where(level == 7, jnp.zeros_like(step), step)
    return direct, jnp.where(level == 0, own_step[:, cut], step)


def ends_next(scal, first, *refs):
    second = refs[:5]
    reflect, e1_ref, e2_ref = refs[5:]
    size = first.shape[1]
    rho = rho_of(scal, reflect[...])
    sign = sign_of(scal)
    for cut in (slice(0, HALO), slice(size - HALO, size)):
        goes_first = (scal[2] == 0) == (cut.start > 0)
        start = 0
        for part in second_parts(scal, *second, cut=cut):
            rows = pl.ds(start, part.shape[0])
            pair = mixed(rho[:, cut], sign, first[rows, cut], part)

            @pl.when(goes_first)
            def _():
                for f in range(2):
                    e1_ref[f, rows, :] = pair[f]

            @pl.when(jnp.logical_not(goes_first))
            def _():
                for f in range(2):
                    e2_ref[f, rows, :] = pair[f]

            start += part.shape[0]


def ends_start(scal, down, up, reflect, e1_ref, e2_ref, ends_ref, r_ref, sems):
    odd = scal[0] == 1
    even_tile = scal[2] == 0
    size = down.shape[2]
    cuts = (slice(0, HALO), slice(size - HALO, size))
    copies = [pltpu.make_async_copy(reflect, r_ref, sems.at[4])]
    for i, state in enumerate((down, up)):
        for j, cut in enumerate(cuts):
            source = state.at[0, :, pl.ds(cut.start, HALO)]
            copies.append(pltpu.make_async_copy(source, ends_ref.at[i, j], sems.at[2 * i + j]))
    for copy in copies:
        copy.start()
    for copy in copies:
        copy.wait()
    rho = rho_of(scal, r_ref[...])
    for j, cut in enumerate(cuts):
        one, two = ends_ref[0, j], ends_ref[1, j]
        pair = mixed(rho[:, cut], 1.0, jnp.where(odd, one, two), jnp.where(odd, two, one))
        goes_first = even_tile == (j == 1)

        @pl.when(goes_first)
        def _():
            for f in range(2):
                e1_ref[f] = pair[f]

        @pl.when(jnp.logical_not(goes_first))
        def _():
            for f in range(2):
                e2_ref[f] = pair[f]


def dot(left, right):
    return jnp.dot(left, right, preferred_element_type=jnp.float32)


def inner_dots(m_ref, w_ref, acc_ref, f):
    columns = m_ref.shape[1]
    left = jnp.concatenate([m_ref[f, :, :BLOCK], m_ref[f, :, BLOCK:]], axis=0)
    both = dot(left, w_ref[f, HALO : HALO + BLOCK, :])
    acc_ref[f, :columns] = both[:columns] + dot(m_ref[f, :, BLOCK : BLOCK + HALO], w_ref[f, HALO + BLOCK :, :])
    acc_ref[f, columns:] = both[columns:] + dot(m_ref[f, :, HALO:BLOCK], w_ref[f, :HALO, :])


def body_start(scal, down, up, reflect, w_down, w_up, acc_ref, w_ref, m_ref, sems):
    odd = scal[0] == 1

    def copies(*sources):
        return [pltpu.make_async_copy(w.at[0, 0], w_ref.at[f], sems.at[f]) for f, w in enumerate(sources)]

    @pl.when(odd)
    def _():
        for copy in copies(w_down, w_up):
            copy.start()

    @pl.when(jnp.logical_not(odd))
    def _():
        for copy in copies(w_up, w_down):
            copy.start()

    one, two = down[0], up[0]
    pair = mixed(rho_of(scal, reflect[...]), 1.0, jnp.where(odd, one, two), jnp.where(odd, two, one))
    for f in range(2):
        m_ref[f] = pair[f]
    for f, copy in enumerate(copies(w_down, w_up)):
        copy.wait()
        inner_dots(m_ref, w_ref, acc_ref, f)


def body_next(scal, first, *refs):
    reflect, w_ref, acc_ref, m_ref = refs[5:]
    rho = rho_of(scal, reflect[...])
    start = 0
    for part in second_parts(scal, *refs[:5]):
        rows = pl.ds(start, part.shape[0])
        pair = mixed(rho, sign_of(scal), first[rows, :], part)
        for f in range(2):
            m_ref[f, rows, :] = pair[f]
        start += part.shape[0]
    for f in range(2):
        inner_dots(m_ref, w_ref, acc_ref, f)


def halo_dots(scal, h1_ref, h2_ref, acc_ref, w_ref, *outs):
    even = scal[2] == 0
    for f, parts in ((0, outs[:2]), (1, outs[2:])):
        h1 = h1_ref[f]
        h2 = h2_ref[f]
        columns = h1.shape[0]
        left = acc_ref[f, :columns] + dot(jnp.where(even, h2, h1), w_ref[f, :HALO, :])
        right = acc_ref[f, columns:] + dot(jnp.where(even, h1, h2), w_ref[f, HALO + BLOCK :, :])
        start = 0
        for out in parts:
            rows = out.shape[0]
            out[:, :BLOCK] = left[start : start + rows].astype(jnp.bfloat16)
            out[:, BLOCK:] = right[start : start + rows].astype(jnp.bfloat16)
            start += rows


def finish(scal, first, *refs):
    down_ref, up_ref = refs[-2:]
    sign = sign_of(scal).astype(jnp.bfloat16)
    odd = scal[0] == 1
    start = 0
    for part in second_parts(scal, *refs[:-2]):
        rows = pl.ds(start, part.shape[0])
        one = first[rows, :]
        two = part * sign
        down_ref[0, rows, :] = jnp.where(odd, one, two)
        up_ref[0, rows, :] = jnp.where(odd, two, one)
        start += part.shape[0]


def on_device(down_state, up_state, reflectivity, w_down, w_up):
    tiles = lax.axis_size("lat")
    columns, wide = down_state.shape[1:]
    inside = swap(*[(i, i + 1) for i in range(0, tiles, 2)])
    outside = swap(*[(i, i + 1) for i in range(1, tiles - 1, 2)])
    far = [pltpu.with_memory_space_constraint(x, pltpu.HBM) for x in (down_state, up_state, reflectivity, w_down, w_up)]
    sums = f32(2, 2 * columns, BLOCK)
    fields = pltpu.VMEM((2, columns, wide), jnp.bfloat16)
    for tick in range(len(STEP_ROWS)):
        if tick == 0:
            e1, e2 = call(
                ends_start,
                (bf(2, columns, HALO),) * 2,
                tuple(far[:3]),
                "ends",
                specs=[HBM] * 3,
                scratch=[
                    pltpu.VMEM((2, 2, columns, HALO), jnp.bfloat16),
                    pltpu.VMEM((1, wide), jnp.float32),
                    pltpu.SemaphoreType.DMA((5,)),
                ],
            )
        else:
            e1, e2 = call(ends_next, (bf(2, columns, HALO),) * 2, (first, *second, reflectivity), "ends")
        h2 = lax.ppermute(e2, "lat", outside)
        h1 = lax.ppermute(e1, "lat", inside)
        if tick == 0:
            acc, weights = call(
                body_start,
                (sums, bf(2, 2 * BLOCK, BLOCK)),
                (down_state, up_state, reflectivity, *far[3:]),
                "body",
                specs=[VMEM] * 3 + [HBM] * 2,
                scratch=[fields, pltpu.SemaphoreType.DMA((2,))],
            )
        else:
            (acc,) = call(body_next, (sums,), (first, *second, reflectivity, weights), "body", scratch=[fields])
        *own, other = call(
            halo_dots,
            (bf(columns - STEP_ROWS[tick], wide), bf(STEP_ROWS[tick], wide), bf(columns, wide)),
            (h1, h2, acc, weights),
            "edges",
        )
        first = lax.ppermute(other, "depth", SECOND)
        got_step = lax.ppermute(own[1], "depth", FIRST_STEP)
        got_direct = lax.ppermute(own[0], "depth", FIRST_DIRECT)
        got_forward = lax.ppermute(got_step, "depth", FIRST_FORWARD)
        second = (*own, got_direct, got_step, got_forward)
    return call(finish, (bf(1, columns, wide),) * 2, (first, *second), "finish")


def solution(mesh):
    in_specs = (
        P("depth", None, "lat"),
        P("depth", None, "lat"),
        P("depth", "lat"),
        P("depth", "lat", None, None),
        P("depth", "lat", None, None),
    )
    out_specs = (P("depth", None, "lat"), P("depth", None, "lat"))
    return jax.shard_map(
        on_device, mesh=mesh, in_specs=in_specs, out_specs=out_specs, check_vma=False
    )
```

```python
import functools

import jax
import jax.numpy as jnp
from jax import lax
from jax.experimental import pallas as pl
from jax.experimental.pallas import tpu as pltpu
from jax.sharding import PartitionSpec as P

BLOCK = 1024
HALO = 512
STEP_ROWS = (80, 64, 64, 80)
GRANT = 20 * 1024 * 1024
HINT = 10_000_000_000

VMEM = pl.BlockSpec(memory_space=pltpu.VMEM)
HBM = pl.BlockSpec(memory_space=pltpu.HBM)


def swap(*pairs):
    return [q for a, b in pairs for q in ((a, b), (b, a))]


INNER = swap((1, 2), (5, 6))
FIRST_DIRECT = INNER + swap((3, 4))
FIRST_STEP = INNER + swap((0, 3), (4, 7))
FIRST_FORWARD = [(0, 4), (7, 3)]
SECOND = swap((0, 1), (2, 3), (4, 5), (6, 7))


def bf(*shape):
    return jax.ShapeDtypeStruct(shape, jnp.bfloat16)


def f32(*shape):
    return jax.ShapeDtypeStruct(shape, jnp.float32)


def call(body, outs, ins, name, specs=None, scratch=(), out_specs=None, aliases=None):
    def kernel(*refs):
        level = lax.axis_index("depth")
        body((level % 2, level, lax.axis_index("lat") % 2), *refs)

    return pl.pallas_call(
        kernel,
        out_shape=tuple(outs),
        in_specs=specs or [VMEM] * len(ins),
        out_specs=out_specs or tuple(VMEM for _ in outs),
        scratch_shapes=scratch,
        input_output_aliases=aliases or {},
        compiler_params=pltpu.CompilerParams(vmem_limit_bytes=GRANT),
        cost_estimate=pl.CostEstimate(flops=HINT, transcendentals=0, bytes_accessed=1),
        name=name,
    )(*ins)


def mixed(rho, sign, first, second):
    first = first.astype(jnp.float32)
    second = second.astype(jnp.float32)
    return (
        ((1.0 + rho) * first - (rho * sign) * second).astype(jnp.bfloat16),
        (((1.0 - rho) * sign) * second + rho * first).astype(jnp.bfloat16),
    )


def rho_of(scal, reflect):
    return reflect * jnp.where(scal[0] == 1, 1.0, -1.0)


def sign_of(scal):
    return jnp.where(scal[1] == 0, -1.0, 1.0)


def second_parts(scal, own_direct, own_step, got_direct, got_step, got_forward, cut=slice(None)):
    level = scal[1]
    direct = jnp.where(level == 0, own_direct[:, cut], got_direct[:, cut])
    step = jnp.where((level == 3) | (level == 4), got_forward[:, cut], got_step[:, cut])
    step = jnp.where(level == 7, jnp.zeros_like(step), step)
    return direct, jnp.where(level == 0, own_step[:, cut], step)


def ends_next(scal, first, *refs):
    second = refs[:5]
    reflect, e1_ref, e2_ref = refs[5:]
    size = first.shape[1]
    rho = rho_of(scal, reflect[...])
    sign = sign_of(scal)
    for cut in (slice(0, HALO), slice(size - HALO, size)):
        goes_first = (scal[2] == 0) == (cut.start > 0)
        start = 0
        for part in second_parts(scal, *second, cut=cut):
            rows = pl.ds(start, part.shape[0])
            pair = mixed(rho[:, cut], sign, first[rows, cut], part)

            @pl.when(goes_first)
            def _():
                for f in range(2):
                    e1_ref[f, rows, :] = pair[f]

            @pl.when(jnp.logical_not(goes_first))
            def _():
                for f in range(2):
                    e2_ref[f, rows, :] = pair[f]

            start += part.shape[0]


def ends_start(scal, down, up, reflect, e1_ref, e2_ref, ends_ref, r_ref, sems):
    odd = scal[0] == 1
    even_tile = scal[2] == 0
    size = down.shape[2]
    cuts = (slice(0, HALO), slice(size - HALO, size))
    copies = [pltpu.make_async_copy(reflect, r_ref, sems.at[4])]
    for i, state in enumerate((down, up)):
        for j, cut in enumerate(cuts):
            source = state.at[0, :, pl.ds(cut.start, HALO)]
            copies.append(pltpu.make_async_copy(source, ends_ref.at[i, j], sems.at[2 * i + j]))
    for copy in copies:
        copy.start()
    for copy in copies:
        copy.wait()
    rho = rho_of(scal, r_ref[...])
    for j, cut in enumerate(cuts):
        one, two = ends_ref[0, j], ends_ref[1, j]
        pair = mixed(rho[:, cut], 1.0, jnp.where(odd, one, two), jnp.where(odd, two, one))
        goes_first = even_tile == (j == 1)

        @pl.when(goes_first)
        def _():
            for f in range(2):
                e1_ref[f] = pair[f]

        @pl.when(jnp.logical_not(goes_first))
        def _():
            for f in range(2):
                e2_ref[f] = pair[f]


def dot(left, right):
    return jnp.dot(left, right, preferred_element_type=jnp.float32)


def inner_dots(m_ref, w_ref, acc_ref, f):
    columns = m_ref.shape[1]
    left = jnp.concatenate([m_ref[f, :, :BLOCK], m_ref[f, :, BLOCK:]], axis=0)
    both = dot(left, w_ref[f, HALO : HALO + BLOCK, :])
    acc_ref[f, :columns] = both[:columns] + dot(m_ref[f, :, BLOCK : BLOCK + HALO], w_ref[f, HALO + BLOCK :, :])
    acc_ref[f, columns:] = both[columns:] + dot(m_ref[f, :, HALO:BLOCK], w_ref[f, :HALO, :])


def body_start(scal, down, up, reflect, w_down, w_up, acc_ref, w_ref, m_ref, sems):
    odd = scal[0] == 1

    def copies(*sources):
        return [pltpu.make_async_copy(w.at[0, 0], w_ref.at[f], sems.at[f]) for f, w in enumerate(sources)]

    @pl.when(odd)
    def _():
        for copy in copies(w_down, w_up):
            copy.start()

    @pl.when(jnp.logical_not(odd))
    def _():
        for copy in copies(w_up, w_down):
            copy.start()

    one, two = down[0], up[0]
    pair = mixed(rho_of(scal, reflect[...]), 1.0, jnp.where(odd, one, two), jnp.where(odd, two, one))
    for f in range(2):
        m_ref[f] = pair[f]
    for f, copy in enumerate(copies(w_down, w_up)):
        copy.wait()
        inner_dots(m_ref, w_ref, acc_ref, f)


def body_next(scal, first, *refs):
    reflect, w_ref, acc_ref, m_ref = refs[5:]
    rho = rho_of(scal, reflect[...])
    start = 0
    for part in second_parts(scal, *refs[:5]):
        rows = pl.ds(start, part.shape[0])
        pair = mixed(rho, sign_of(scal), first[rows, :], part)
        for f in range(2):
            m_ref[f, rows, :] = pair[f]
        start += part.shape[0]
    for f in range(2):
        inner_dots(m_ref, w_ref, acc_ref, f)


def halo_dots(scal, h1_ref, h2_ref, acc_ref, w_ref, *outs):
    even = scal[2] == 0
    for f, parts in ((0, outs[:2]), (1, outs[2:])):
        h1 = h1_ref[f]
        h2 = h2_ref[f]
        columns = h1.shape[0]
        left = acc_ref[f, :columns] + dot(jnp.where(even, h2, h1), w_ref[f, :HALO, :])
        right = acc_ref[f, columns:] + dot(jnp.where(even, h1, h2), w_ref[f, HALO + BLOCK :, :])
        start = 0
        for out in parts:
            rows = out.shape[0]
            out[:, :BLOCK] = left[start : start + rows].astype(jnp.bfloat16)
            out[:, BLOCK:] = right[start : start + rows].astype(jnp.bfloat16)
            start += rows


def finish(scal, first, *refs):
    down_ref, up_ref = refs[-2:]
    sign = sign_of(scal).astype(jnp.bfloat16)
    odd = scal[0] == 1
    start = 0
    for part in second_parts(scal, *refs[:-2]):
        rows = pl.ds(start, part.shape[0])
        one = first[rows, :]
        two = part * sign
        down_ref[0, rows, :] = jnp.where(odd, one, two)
        up_ref[0, rows, :] = jnp.where(odd, two, one)
        start += part.shape[0]


def on_device(down_state, up_state, reflectivity, w_down, w_up):
    tiles = lax.axis_size("lat")
    columns, wide = down_state.shape[1:]
    inside = swap(*[(i, i + 1) for i in range(0, tiles, 2)])
    outside = swap(*[(i, i + 1) for i in range(1, tiles - 1, 2)])
    far = [pltpu.with_memory_space_constraint(x, pltpu.HBM) for x in (down_state, up_state, reflectivity, w_down, w_up)]
    sums = f32(2, 2 * columns, BLOCK)
    fields = pltpu.VMEM((2, columns, wide), jnp.bfloat16)
    for tick in range(len(STEP_ROWS)):
        if tick == 0:
            e1, e2 = call(
                ends_start,
                (bf(2, columns, HALO),) * 2,
                tuple(far[:3]),
                "ends",
                specs=[HBM] * 3,
                scratch=[
                    pltpu.VMEM((2, 2, columns, HALO), jnp.bfloat16),
                    pltpu.VMEM((1, wide), jnp.float32),
                    pltpu.SemaphoreType.DMA((5,)),
                ],
            )
        else:
            e1, e2 = call(ends_next, (bf(2, columns, HALO),) * 2, (first, *second, reflectivity), "ends")
        h2 = lax.ppermute(e2, "lat", outside)
        h1 = lax.ppermute(e1, "lat", inside)
        if tick == 0:
            acc, weights = call(
                body_start,
                (sums, bf(2, 2 * BLOCK, BLOCK)),
                (down_state, up_state, reflectivity, *far[3:]),
                "body",
                specs=[VMEM] * 3 + [HBM] * 2,
                scratch=[fields, pltpu.SemaphoreType.DMA((2,))],
            )
        else:
            (acc,) = call(body_next, (sums,), (first, *second, reflectivity, weights), "body", scratch=[fields])
        *own, other = call(
            halo_dots,
            (bf(columns - STEP_ROWS[tick], wide), bf(STEP_ROWS[tick], wide), bf(columns, wide)),
            (h1, h2, acc, weights),
            "edges",
        )
        first = lax.ppermute(other, "depth", SECOND)
        got_step = lax.ppermute(own[1], "depth", FIRST_STEP)
        got_direct = lax.ppermute(own[0], "depth", FIRST_DIRECT)
        got_forward = lax.ppermute(got_step, "depth", FIRST_FORWARD)
        second = (*own, got_direct, got_step, got_forward)
    return call(finish, (bf(1, columns, wide),) * 2, (first, *second), "finish")


def solution(mesh):
    in_specs = (
        P("depth", None, "lat"),
        P("depth", None, "lat"),
        P("depth", "lat"),
        P("depth", "lat", None, None),
        P("depth", "lat", None, None),
    )
    out_specs = (P("depth", None, "lat"), P("depth", None, "lat"))
    return jax.shard_map(
        on_device, mesh=mesh, in_specs=in_specs, out_specs=out_specs, check_vma=False
    )
```
